128 devices in a mesh: occ: 8 (over y, core), vir: 16 (over x, z).
Axes of the slice: x: 4, y: 4, z: 4, core: 2. Of those that a mesh axis runs over, the one named last changes fastest.
Arguments:
- amplitudes: bfloat16 [4096, 49152], P('occ', 'vir'), may hold values from -6 to 6
- integral_tiles: bfloat16 [16, 256, 128, 128], P('vir', 'occ'), may hold values from -0.0625 to 0.0625
- tile_cd: int32 [16, 256], replicated, may hold values from 0 to 23, as said below
- tile_ab: int32 [16, 256], replicated, may hold values from 0 to 63, as said below
- slot_tile: int32 [64], replicated, may hold values from 0 to 63, as said below
- residual_in: float32 [4096, 8192], P('occ', 'vir'), may hold values from -6 to 6
- occ_level: float32 [4096], P('occ'), may hold values from -3 to -1
- vir_level: float32 [8192], P('vir'), may hold values from 0.5 to 3
Outputs:
- update: float32 [4096, 8192], P('occ', 'vir')
The draws below stay inside these ranges and needn't reach their ends.
Inputs may be any that keep to these rules, and one draw needn't show every extreme that they name: `tile_cd`: within a group no pair of contracted tile and slab tile repeats. `tile_ab`: for every group and every index w of vir, the group's tiles name slab tiles held in exactly 2 of the slots w * 4 to (w + 1) * 4 - 1. `slot_tile`: A permutation of the slab tiles.
All inputs are finite; a program needn't handle non-finite values.
Results may differ from the reference program's by a relative error of at most 0.0003.
Values may be sent and summed in bfloat16 or wider, within the bound.
A program may use at most 128 MiB of HBM per device.

```python
import jax
import jax.numpy as jnp
from jax import lax

TILE = 128
KT_DEV = 24
QT_DEV = 4
CAP = 2
OPAIRS = 4096
NK = 384
NQ = 64
GROUPS = 16
TILES_GROUP = 256


def group_list(key, reach):
    width = GROUPS * CAP
    places = KT_DEV * width
    cover_kind = jax.random.randint(jax.random.fold_in(key, 1), (width,), 0, KT_DEV).astype(jnp.int32)
    scores = jax.random.permutation(jax.random.fold_in(key, 2), places).astype(jnp.int32)
    steps = jnp.arange(width, dtype=jnp.int32)
    scores = scores.at[cover_kind * width + steps].set(-1 - steps)
    picked = jnp.argsort(scores, stable=True)[:TILES_GROUP].astype(jnp.int32)
    mixing = jax.random.permutation(jax.random.fold_in(key, 3), TILES_GROUP)
    picked = picked[mixing]
    return ((picked // width).astype(jnp.int32), reach[picked % width])


def shared_lists(key):
    order = jax.random.permutation(jax.random.fold_in(key, 11), NQ).astype(jnp.int32)
    pick_keys = jax.random.split(jax.random.fold_in(key, 12), GROUPS * GROUPS)
    picks = jax.vmap(lambda k: jax.random.permutation(k, QT_DEV)[:CAP])(pick_keys)
    picks = picks.reshape(GROUPS, GROUPS, CAP).astype(jnp.int32)
    owners = jnp.arange(GROUPS, dtype=jnp.int32)[None, :, None]
    reached = (owners * QT_DEV + picks).reshape(GROUPS, GROUPS * CAP)
    group_keys = jax.random.split(jax.random.fold_in(key, 14), GROUPS)
    kinds, slots = jax.vmap(group_list)(group_keys, reached)
    return (order, order[slots], kinds)


def draw_tile_ab(key, part):
    return shared_lists(key)[1]


def draw_slot_tile(key, part):
    return shared_lists(key)[0]


def draw_tile_cd(key, part):
    return shared_lists(key)[2]


def shard_levels(stream_key, extent, cuts, least, high):
    factor_of, own = 1.0, jax.random.fold_in(stream_key, 6)
    for dim, blocks in cuts:
        draws = jnp.exp(jax.random.uniform(jax.random.fold_in(own, dim), (blocks,), jnp.float32, least / len(cuts), high / len(cuts)))
        factor_of = factor_of * jnp.repeat(draws, extent[dim] // blocks).reshape([-1 if axis == dim else 1 for axis in range(len(extent))])
    return factor_of


def gaussian(own_key, shape, scale, most, cuts=(), held_as=jnp.bfloat16):
    loudness = shard_levels(own_key, shape, cuts, -0.22, 0.18) if cuts else 1.0
    values = jax.random.normal(own_key, shape, jnp.float32) * scale * loudness
    return jnp.minimum(jnp.maximum(values, -most), most).astype(held_as)


def setup_inputs(seed: int = 0) -> dict:
    arg_keys = jax.random.split(jax.random.key(seed), 9)
    amplitudes = gaussian(arg_keys[0], (OPAIRS, NK * TILE), 1.0, 6.0, ((0, 8), (1, 16)))
    integral_tiles = gaussian(arg_keys[1], (GROUPS, TILES_GROUP, TILE, TILE), (TILE * TILES_GROUP // QT_DEV) ** -0.5, 0.0625, ((0, 16), (1, 8)))
    tile_cd = draw_tile_cd(jax.random.fold_in(arg_keys[8], 71), 0)
    tile_ab = draw_tile_ab(jax.random.fold_in(arg_keys[8], 71), 0)
    slot_tile = draw_slot_tile(jax.random.fold_in(arg_keys[8], 71), 0)
    residual_in = gaussian(arg_keys[5], (OPAIRS, NQ * TILE), 1.0, 6.0, ((0, 8), (1, 16)), jnp.float32)
    occ_level = jnp.clip(-3.0 + 2.0 * jax.random.uniform(arg_keys[6], (OPAIRS,), jnp.float32) ** shard_levels(arg_keys[6], (OPAIRS,), ((0, 8),), -0.2, 0.2), -3.0, -1.0)
    vir_level = jnp.clip(0.5 + 2.5 * jax.random.uniform(arg_keys[7], (NQ * TILE,), jnp.float32) ** shard_levels(arg_keys[7], (NQ * TILE,), ((0, 16),), -0.2, 0.2), 0.5, 3.0)
    return dict(amplitudes=amplitudes, integral_tiles=integral_tiles, tile_cd=tile_cd, tile_ab=tile_ab, slot_tile=slot_tile, residual_in=residual_in, occ_level=occ_level, vir_level=vir_level)


def reference(amplitudes, integral_tiles, tile_cd, tile_ab, slot_tile, residual_in, occ_level, vir_level):
    def one_group(total, group):
        start = (group * KT_DEV * TILE).astype(jnp.int32)
        columns = lax.dynamic_slice_in_dim(amplitudes, start, KT_DEV * TILE, 1).astype(jnp.float32)
        tiles = lax.dynamic_index_in_dim(integral_tiles, group, 0, keepdims=False).astype(jnp.float32)
        kinds = lax.dynamic_index_in_dim(tile_cd, group, 0, keepdims=False)
        targets = lax.dynamic_index_in_dim(tile_ab, group, 0, keepdims=False)
        dense = jnp.zeros((KT_DEV, NQ, TILE, TILE), jnp.float32).at[kinds, targets].add(tiles)
        dense = dense.transpose(0, 2, 1, 3).reshape(KT_DEV * TILE, NQ * TILE)
        return total + jnp.dot(columns, dense, precision=lax.Precision.HIGHEST), None

    ladder, _ = lax.scan(one_group, jnp.zeros((OPAIRS, NQ * TILE), jnp.float32), jnp.arange(GROUPS, dtype=jnp.int32))
    by_slot = ladder.reshape(OPAIRS, NQ, TILE)[:, slot_tile].reshape(OPAIRS, NQ * TILE)
    return (residual_in + by_slot) / (occ_level[:, None] - vir_level[None, :])
```

```python
import jax
import jax.numpy as jnp
from jax import lax
from jax.experimental import pallas as pl
from jax.experimental.pallas import tpu as pltpu
from jax.sharding import PartitionSpec as P

CAP = 2
TILE = 128
MESH = pl.DeviceIdType.MESH
PIECES = 4
FULL = 32767.0

ORDER = (
    (2, 2), (2, 1), (1, 2), (2, 3), (3, 2), (2, 0), (0, 2), (1, 1),
    (3, 3), (1, 3), (3, 1), (1, 0), (3, 0), (0, 1), (0, 3), (0, 0),
)


def pick(i, values):
    out = jnp.int32(values[0])
    for n, v in enumerate(values[1:], 1):
        out = jnp.where(i == n, jnp.int32(v), out)
    return out


def code(v):
    top = jnp.maximum(jnp.max(jnp.abs(v), axis=0, keepdims=True), 1e-30)
    return jnp.round(v * (FULL / top)).astype(jnp.int32).astype(jnp.int16), top * (1.0 / FULL)


def kernel(
    table, chosen, amp_hbm, tiles_hbm, out,
    amp, pool, q1s, u1s, q1r, u1r, q2s, u2s, q2r, u2r, own, total,
    amp_sem, local_sem, gs_send, gs_recv, q1_send, q1_recv, u1_send, u1_recv, q2_send, q2_recv, u2_send, u2_recv,
):
    occ, vir = lax.axis_index("occ"), lax.axis_index("vir")
    y, core = occ // 2, occ % 2
    x, z = vir // 4, vir % 4
    up = (((y + 1) % 4) * 2 + core, vir)
    down = (((y + 3) % 4) * 2 + core, vir)
    mate = (y * 2 + 1 - core, vir)
    at_x = [(occ, ((x + d) % 4) * 4 + z) for d in range(4)]
    at_z = [(occ, x * 4 + (z + d) % 4) for d in range(4)]
    own_tiles = tiles_hbm.shape[0]
    part = own_tiles // PIECES
    kinds = amp_hbm.shape[1] // TILE
    half = amp_hbm.shape[0] // 2

    load_amp = pltpu.make_async_copy(amp_hbm, amp, amp_sem)
    load_amp.start()

    barrier = pltpu.get_barrier_semaphore()
    greeted = [up, down, mate] + at_x[1:] + at_z[1:]
    for other in greeted:
        pl.semaphore_signal(barrier, inc=1, device_id=other, device_id_type=MESH)
    pl.semaphore_wait(barrier, len(greeted))

    def place(yy, cc, piece):
        return pool.at[pl.ds(((yy % 4) * 2 + cc) * own_tiles + piece * part, part)]

    def mine(piece):
        return tiles_hbm.at[pl.ds(piece * part, part)]

    def send(kind, piece, source, target, device):
        return pltpu.make_async_remote_copy(
            src_ref=source, dst_ref=target, send_sem=gs_send.at[kind, piece],
            recv_sem=gs_recv.at[kind, piece], device_id=device, device_id_type=MESH,
        )

    pieces = range(PIECES)
    low, high = pieces[: PIECES // 2], pieces[PIECES // 2 :]
    first_up = [send(0, p, mine(p), place(y, core, p), up) for p in pieces]
    first_down = [send(1, p, mine(p), place(y, core, p), down) for p in pieces]
    to_mate = [send(3, p, mine(p), place(y, core, p), mate) for p in pieces]
    here = [pltpu.make_async_copy(mine(p), place(y, core, p), local_sem.at[p]) for p in pieces]
    for a, b in zip(pieces, list(high) + list(low)):
        first_up[a].start()
        first_down[b].start()
    for p in pieces:
        to_mate[p].start()
        here[p].start()
    pool[pool.shape[0] - 1] = jnp.zeros((TILE, TILE), pool.dtype)
    passed, relayed = {}, {}

    def relay(kind, p, yy):
        relayed[kind, p] = send(kind, p, place(yy, core, p), place(yy, core, p), mate)
        relayed[kind, p].start()

    for a, b in zip(pieces, list(high) + list(low)):
        first_up[a].wait_recv()
        if a in low:
            passed[a] = send(2, a, place(y + 3, core, a), place(y + 3, core, a), up)
            passed[a].start()
        first_down[b].wait_recv()
        if b in high:
            passed[b] = send(2, b, place(y + 1, core, b), place(y + 1, core, b), down)
            passed[b].start()
        relay(4, a, y + 3)
        relay(5, b, y + 1)
    for a, b in zip(low, high):
        for p in (a, b):
            passed[p].wait_recv()
            relay(6, p, y + 2)
    load_amp.wait()
    for p in pieces:
        here[p].wait()
        to_mate[p].wait_recv()
        relayed[4, p].wait_recv()
        relayed[5, p].wait_recv()
    for a, b in zip(low, high):
        relayed[6, a].wait_recv()
        relayed[6, b].wait_recv()

    def first_leg(h, d, e):
        device = (occ, ((x + d) % 4) * 4 + z) if h == 0 else (occ, x * 4 + (z + d) % 4)
        return [
            pltpu.make_async_remote_copy(
                src_ref=s.at[h, d, e], dst_ref=r.at[h, d, e], send_sem=ss.at[h, d, e],
                recv_sem=rs.at[h, d, e], device_id=device, device_id_type=MESH,
            )
            for s, r, ss, rs in ((q1s, q1r, q1_send, q1_recv), (u1s, u1r, u1_send, u1_recv))
        ]

    rows4 = lax.broadcasted_iota(jnp.int32, (4, TILE), 0)

    def one_owner(i, carry):
        dx, dz = pick(i, [o[0] for o in ORDER]), pick(i, [o[1] for o in ORDER])
        owner = ((x + dx) % 4) * 4 + (z + dz) % 4
        places = [chosen[owner * CAP + b] for b in range(CAP)]
        starts = [(owner * 4 + place) * kinds for place in places]
        value = jnp.zeros((2 * half, CAP * TILE), jnp.float32)
        for k in range(0, kinds, 2):
            rhs = jnp.concatenate(
                [
                    jnp.concatenate([pool[table[starts[b] + kk]] for b in range(CAP)], axis=1)
                    for kk in (k, k + 1)
                ],
                axis=0,
            )
            value = value + jnp.dot(
                amp[:, k * TILE : (k + 2) * TILE], rhs, preferred_element_type=jnp.float32
            )
        for h, d, e in ((0, dx, dz), (1, dz, dx)):
            units = []
            for b in range(CAP):
                q, unit = code(value[h * half : (h + 1) * half, b * TILE : (b + 1) * TILE])
                q1s[h, d, e, b] = q
                units.append(jnp.where(rows4 == places[b], unit, 0.0))
            u1s[h, d, e] = jnp.concatenate(units, axis=0)

            @pl.when(d != 0)
            def _():
                for copy in first_leg(h, d, e):
                    copy.start()

        return carry

    lax.fori_loop(0, len(ORDER), one_owner, 0)

    def second_leg(h, e):
        device = at_z[e] if h == 0 else at_x[e]
        return [
            pltpu.make_async_remote_copy(
                src_ref=s.at[h, e], dst_ref=r.at[h, e], send_sem=ss.at[h, e],
                recv_sem=rs.at[h, e], device_id=device, device_id_type=MESH,
            )
            for s, r, ss, rs in ((q2s, q2r, q2_send, q2_recv), (u2s, u2r, u2_send, u2_recv))
        ]

    step = 64

    def add_up(h, e, into):
        for d in range(1, 4):
            for copy in first_leg(h, d, e):
                copy.wait_recv()

        def some_rows(n, carry):
            span = pl.ds(pl.multiple_of(n * step, step), step)
            sums = [jnp.zeros((step, TILE), jnp.float32) for _ in range(4)]
            for d in range(4):
                q_ref, u_ref = (q1s, u1s) if d == 0 else (q1r, u1r)
                for b in range(CAP):
                    v = q_ref[h, d, e, b, span].astype(jnp.int32).astype(jnp.float32)
                    for j in range(4):
                        row = b * 4 + j
                        sums[j] = sums[j] + v * u_ref[h, d, e, row : row + 1]
            for j in range(4):
                into[j, span] = sums[j]
            return carry

        lax.fori_loop(0, half // step, some_rows, 0)

    for e in (2, 1, 3):
        for h in range(2):
            add_up(h, e, total)
            units = []
            for j in range(4):
                q, unit = code(total[j])
                q2s[h, e, j] = q
                units.append(unit)
            u2s[h, e] = jnp.concatenate(units + units, axis=0)
            for copy in second_leg(h, e):
                copy.start()
    for h in range(2):
        add_up(h, 0, own.at[h])
    for h in range(2):
        for e in (2, 1, 3):
            for copy in second_leg(h, e):
                copy.wait_recv()

    for h in range(2):

        def finish(n, carry):
            span = pl.ds(pl.multiple_of(n * step, step), step)
            rows = pl.ds(pl.multiple_of(h * half + n * step, step), step)
            for j in range(4):
                v = own[h, j, span]
                for e in (1, 2, 3):
                    v = v + q2r[h, e, j, span].astype(jnp.int32).astype(jnp.float32) * u2r[h, e, j : j + 1]
                out[rows, j * TILE : (j + 1) * TILE] = v
            return carry

        lax.fori_loop(0, half // step, finish, 0)

    for copy in first_up + first_down + to_mate + list(passed.values()) + list(relayed.values()):
        copy.wait_send()
    for h in range(2):
        for e in range(4):
            for d in range(1, 4):
                for copy in first_leg(h, d, e):
                    copy.wait_send()
            if e:
                for copy in second_leg(h, e):
                    copy.wait_send()


def ladder(table, chosen, amplitudes, tiles):
    rows = amplitudes.shape[0]
    half, every = rows // 2, tiles.shape[0] * 8
    vm, dma = pltpu.VMEM, pltpu.SemaphoreType.DMA
    first_q, first_u = (2, 4, 4, CAP, half, TILE), (2, 4, 4, 8, TILE)
    second_q, second_u = (2, 4, 4, half, TILE), (2, 4, 8, TILE)
    return pl.pallas_call(
        kernel,
        out_shape=jax.ShapeDtypeStruct((rows, 4 * TILE), jnp.float32),
        in_specs=[pl.BlockSpec(memory_space=pltpu.SMEM)] * 2 + [pl.BlockSpec(memory_space=pl.ANY)] * 2,
        out_specs=pl.BlockSpec(memory_space=pltpu.VMEM),
        scratch_shapes=[
            vm(amplitudes.shape, jnp.bfloat16),
            vm((every + 1, TILE, TILE), jnp.bfloat16),
            vm(first_q, jnp.int16), vm(first_u, jnp.float32), vm(first_q, jnp.int16), vm(first_u, jnp.float32),
            vm(second_q, jnp.int16), vm(second_u, jnp.float32), vm(second_q, jnp.int16), vm(second_u, jnp.float32),
            vm((2, 4, half, TILE), jnp.float32), vm((4, half, TILE), jnp.float32),
            dma, dma((PIECES,)), dma((7, PIECES)), dma((7, PIECES)),
            dma((2, 4, 4)), dma((2, 4, 4)), dma((2, 4, 4)), dma((2, 4, 4)),
            dma((2, 4)), dma((2, 4)), dma((2, 4)), dma((2, 4)),
        ],
        compiler_params=pltpu.CompilerParams(
            collective_id=0, has_side_effects=True, vmem_limit_bytes=56 * 2**20
        ),
    )(table, chosen, amplitudes, tiles)


def shards(
    amplitudes, integral_tiles, tile_cd, tile_ab, slot_tile, residual_in, occ_level, vir_level
):
    mine = lax.axis_index("vir")
    kinds = amplitudes.shape[1] // TILE
    count = tile_cd.shape[1]
    my_kinds = lax.dynamic_index_in_dim(tile_cd, mine, 0, keepdims=False)
    my_tiles = lax.dynamic_index_in_dim(tile_ab, mine, 0, keepdims=False)
    match = slot_tile[:, None] == my_tiles[None, :]
    number = jnp.arange(1, count + 1, dtype=jnp.float32)[:, None]
    of_kind = jnp.where(my_kinds[:, None] == jnp.arange(kinds, dtype=jnp.int32), number, 0.0)
    named = jnp.dot(match.astype(jnp.float32), of_kind, precision=lax.Precision.HIGHEST).astype(jnp.int32)
    table = jnp.where(named == 0, count, named - 1).reshape(-1)
    r = jnp.any(match, axis=1).reshape(-1, 4)
    least = jnp.where(r[:, 0], 0, jnp.where(r[:, 1], 1, 2))
    most = jnp.where(r[:, 3], 3, jnp.where(r[:, 2], 2, 1))
    chosen = jnp.stack([least, most], axis=1).astype(jnp.int32).reshape(-1)
    by_slot = ladder(table, chosen, amplitudes, integral_tiles[0])
    return (residual_in + by_slot) / (occ_level[:, None] - vir_level[None, :])


def solution(mesh):
    in_specs = (
        P("occ", "vir"),
        P("vir", "occ", None, None),
        P(),
        P(),
        P(),
        P("occ", "vir"),
        P("occ"),
        P("vir"),
    )
    out_specs = P("occ", "vir")
    return jax.shard_map(shards, mesh=mesh, in_specs=in_specs, out_specs=out_specs, check_vma=False)
```

```python
import functools

import jax
import jax.numpy as jnp
from jax import lax
from jax.experimental import pallas as pl
from jax.experimental.pallas import tpu as pltpu
from jax.sharding import PartitionSpec as P

CAP = 2
TILE = 128
MESH = pl.DeviceIdType.MESH
PIECES = 8
AHEAD = 2
FULL = 32767.0

ORDER = (
    (2, 2), (2, 1), (1, 2), (2, 3), (3, 2), (2, 0), (0, 2), (1, 1),
    (3, 3), (1, 3), (3, 1), (1, 0), (3, 0), (0, 1), (0, 3), (0, 0),
)
EARLY = (3, 4, 4, 5, 6, 6, 7, 7, 8, 8, 8, 8, 8, 8, 8, 8)
LATE = (8,) * 16


def pick(i, values):
    out = jnp.int32(values[0])
    for n, v in enumerate(values[1:], 1):
        out = jnp.where(i == n, jnp.int32(v), out)
    return out


def code(v):
    top = jnp.maximum(jnp.max(jnp.abs(v), axis=0, keepdims=True), 1e-30)
    return jnp.round(v * (FULL / top)).astype(jnp.int32).astype(jnp.int16), top * (1.0 / FULL)


def kernel(
    need, table, chosen, sorting, amp_hbm, tiles_ref, out,
    amp, sorted_tiles, land, pool, q1s, u1s, q1r, u1r, q2s, u2s, q2r, u2r, own, total,
    amp_sem, gs_send, gs_recv, q1_send, q1_recv, u1_send, u1_recv, q2_send, q2_recv, u2_send, u2_recv,
):
    occ, vir = lax.axis_index("occ"), lax.axis_index("vir")
    y, core = occ // 2, occ % 2
    x, z = vir // 4, vir % 4
    up = (((y + 1) % 4) * 2 + core, vir)
    down = (((y + 3) % 4) * 2 + core, vir)
    mate = (y * 2 + 1 - core, vir)
    at_x = [(occ, ((x + d) % 4) * 4 + z) for d in range(4)]
    at_z = [(occ, x * 4 + (z + d) % 4) for d in range(4)]
    own_tiles = tiles_ref.shape[0]
    part = own_tiles // PIECES
    kinds = amp_hbm.shape[1] // TILE
    half = amp_hbm.shape[0] // 2

    load_amp = pltpu.make_async_copy(amp_hbm, amp, amp_sem)
    load_amp.start()

    barrier = pltpu.get_barrier_semaphore()
    greeted = [up, down, mate] + at_x[1:] + at_z[1:]
    for other in greeted:
        pl.semaphore_signal(barrier, inc=1, device_id=other, device_id_type=MESH)
    for n in range(own_tiles):
        sorted_tiles[n] = tiles_ref[sorting[n]]
    pool[pool.shape[0] - 1] = jnp.zeros((TILE, TILE), pool.dtype)
    pl.semaphore_wait(barrier, len(greeted))

    def place(yy, cc, piece, first=0, size=part):
        return land[piece].at[pl.ds(((yy % 4) * 2 + cc) * part + first, size)]

    def send(kind, piece, source, target, device):
        return pltpu.make_async_remote_copy(
            src_ref=source, dst_ref=target, send_sem=gs_send.at[kind, piece],
            recv_sem=gs_recv.at[kind, piece], device_id=device, device_id_type=MESH,
        )

    pieces = range(PIECES)
    mid = part // 2

    def mine(p):
        return sorted_tiles.at[pl.ds(p * part, part)]

    def pass_on(kind, p, yy, first, device):
        spot = place(yy, core, p, first, mid)
        return send(kind, p, spot, spot, device)

    def relay(kind, p, yy):
        return send(kind, p, place(yy, core, p), place(yy, core, p), mate)

    first_up = [send(0, p, mine(p), place(y, core, p), up) for p in pieces]
    first_down = [send(1, p, mine(p), place(y, core, p), down) for p in pieces]
    on_up = [pass_on(2, p, y + 3, 0, up) for p in pieces]
    on_down = [pass_on(3, p, y + 1, mid, down) for p in pieces]
    to_mate = [send(4, p, mine(p), place(y, core, p), mate) for p in pieces]
    low_mate = [relay(5, p, y + 3) for p in pieces]
    high_mate = [relay(6, p, y + 1) for p in pieces]
    far_mate = [relay(7, p, y + 2) for p in pieces]

    def own_piece(p):
        first_up[p].start()
        first_down[p].start()
        to_mate[p].start()

    def arrive(p):
        first_up[p].wait_recv()
        on_up[p].start()
        low_mate[p].start()
        first_down[p].wait_recv()
        on_down[p].start()
        high_mate[p].start()
        if p + AHEAD < PIECES:
            own_piece(p + AHEAD)

    def arrive_far(p):
        on_up[p].wait_recv()
        on_down[p].wait_recv()
        far_mate[p].start()

    def complete(p):
        for copies in (to_mate, low_mate, high_mate, far_mate):
            copies[p].wait_recv()
        base = p * part * 8
        for n in range(8):
            pool[pl.ds(base + n * part, part)] = land[p][pl.ds(n * part, part)]
        pool[pl.ds(base + occ * part, part)] = sorted_tiles[pl.ds(p * part, part)]

    def first_leg(h, d, e):
        device = (occ, ((x + d) % 4) * 4 + z) if h == 0 else (occ, x * 4 + (z + d) % 4)
        return [
            pltpu.make_async_remote_copy(
                src_ref=s.at[h, d, e], dst_ref=r.at[h, d, e], send_sem=ss.at[h, d, e],
                recv_sem=rs.at[h, d, e], device_id=device, device_id_type=MESH,
            )
            for s, r, ss, rs in ((q1s, q1r, q1_send, q1_recv), (u1s, u1r, u1_send, u1_recv))
        ]

    rows4 = lax.broadcasted_iota(jnp.int32, (4, TILE), 0)

    def one_owner(i, carry):
        dx, dz = pick(i, [o[0] for o in ORDER]), pick(i, [o[1] for o in ORDER])
        owner = ((x + dx) % 4) * 4 + (z + dz) % 4
        places = [chosen[owner * CAP + b] for b in range(CAP)]
        starts = [(owner * 4 + place) * kinds for place in places]
        value = jnp.zeros((2 * half, CAP * TILE), jnp.float32)
        for k in range(0, kinds, 2):
            rhs = jnp.concatenate(
                [
                    jnp.concatenate([pool[table[starts[b] + kk]] for b in range(CAP)], axis=1)
                    for kk in (k, k + 1)
                ],
                axis=0,
            )
            value = value + jnp.dot(
                amp[:, k * TILE : (k + 2) * TILE], rhs, preferred_element_type=jnp.float32
            )
        for h, d, e in ((0, dx, dz), (1, dz, dx)):
            units = []
            for b in range(CAP):
                q, unit = code(value[h * half : (h + 1) * half, b * TILE : (b + 1) * TILE])
                q1s[h, d, e, b] = q
                units.append(jnp.where(rows4 == places[b], unit, 0.0))
            u1s[h, d, e] = jnp.concatenate(units, axis=0)

            @pl.when(d != 0)
            def _():
                for copy in first_leg(h, d, e):
                    copy.start()

        return carry

    def owners(available):
        ready = [i for i, n in enumerate(need) if n == available]
        if ready:
            lax.fori_loop(ready[0], ready[-1] + 1, one_owner, 0)

    def second_leg(h, e):
        device = at_z[e] if h == 0 else at_x[e]
        return [
            pltpu.make_async_remote_copy(
                src_ref=s.at[h, e], dst_ref=r.at[h, e], send_sem=ss.at[h, e],
                recv_sem=rs.at[h, e], device_id=device, device_id_type=MESH,
            )
            for s, r, ss, rs in ((q2s, q2r, q2_send, q2_recv), (u2s, u2r, u2_send, u2_recv))
        ]

    step = 64

    def add_up(h, e, into):
        for d in range(1, 4):
            for copy in first_leg(h, d, e):
                copy.wait_recv()

        def some_rows(n, carry):
            span = pl.ds(pl.multiple_of(n * step, step), step)
            sums = [jnp.zeros((step, TILE), jnp.float32) for _ in range(4)]
            for d in range(4):
                q_ref, u_ref = (q1s, u1s) if d == 0 else (q1r, u1r)
                for b in range(CAP):
                    v = q_ref[h, d, e, b, span].astype(jnp.int32).astype(jnp.float32)
                    for j in range(4):
                        row = b * 4 + j
                        sums[j] = sums[j] + v * u_ref[h, d, e, row : row + 1]
            for j in range(4):
                into[j, span] = sums[j]
            return carry

        lax.fori_loop(0, half // step, some_rows, 0)

    def second(e):
        for h in range(2):
            add_up(h, e, total)
            units = []
            for j in range(4):
                q, unit = code(total[j])
                q2s[h, e, j] = q
                units.append(unit)
            u2s[h, e] = jnp.concatenate(units + units, axis=0)
            for copy in second_leg(h, e):
                copy.start()

    for p in range(AHEAD):
        own_piece(p)
    for p in pieces:
        arrive(p)
        if p == 0:
            load_amp.wait()
        else:
            arrive_far(p - 1)
            complete(p - 1)
            owners(p)
    arrive_far(PIECES - 1)
    if need[6] < PIECES:
        second(2)
    complete(PIECES - 1)
    owners(PIECES)
    if need[6] == PIECES:
        second(2)
    second(1)
    second(3)
    for h in range(2):
        add_up(h, 0, own.at[h])
    for h in range(2):
        for e in (2, 1, 3):
            for copy in second_leg(h, e):
                copy.wait_recv()

    for h in range(2):

        def finish(n, carry):
            span = pl.ds(pl.multiple_of(n * step, step), step)
            rows = pl.ds(pl.multiple_of(h * half + n * step, step), step)
            for j in range(4):
                v = own[h, j, span]
                for e in (1, 2, 3):
                    v = v + q2r[h, e, j, span].astype(jnp.int32).astype(jnp.float32) * u2r[h, e, j : j + 1]
                out[rows, j * TILE : (j + 1) * TILE] = v
            return carry

        lax.fori_loop(0, half // step, finish, 0)

    for copies in (first_up, first_down, on_up, on_down, to_mate, low_mate, high_mate, far_mate):
        for copy in copies:
            copy.wait_send()
    for h in range(2):
        for e in range(4):
            for d in range(1, 4):
                for copy in first_leg(h, d, e):
                    copy.wait_send()
            if e:
                for copy in second_leg(h, e):
                    copy.wait_send()


def ladder(need, barrier_id, table, chosen, sorting, amplitudes, tiles):
    rows = amplitudes.shape[0]
    half, every = rows // 2, tiles.shape[0] * 8
    vm, dma = pltpu.VMEM, pltpu.SemaphoreType.DMA
    first_q, first_u = (2, 4, 4, CAP, half, TILE), (2, 4, 4, 8, TILE)
    second_q, second_u = (2, 4, 4, half, TILE), (2, 4, 8, TILE)
    return pl.pallas_call(
        functools.partial(kernel, need),
        out_shape=jax.ShapeDtypeStruct((rows, 4 * TILE), jnp.float32),
        in_specs=[pl.BlockSpec(memory_space=pltpu.SMEM)] * 3
        + [pl.BlockSpec(memory_space=pl.ANY), pl.BlockSpec(memory_space=pltpu.VMEM)],
        out_specs=pl.BlockSpec(memory_space=pltpu.VMEM),
        scratch_shapes=[
            vm(amplitudes.shape, jnp.bfloat16),
            vm(tiles.shape, jnp.bfloat16),
            [vm((every // PIECES, TILE, TILE), jnp.bfloat16) for _ in range(PIECES)],
            vm((every + 1, TILE, TILE), jnp.bfloat16),
            vm(first_q, jnp.int16), vm(first_u, jnp.float32), vm(first_q, jnp.int16), vm(first_u, jnp.float32),
            vm(second_q, jnp.int16), vm(second_u, jnp.float32), vm(second_q, jnp.int16), vm(second_u, jnp.float32),
            vm((2, 4, half, TILE), jnp.float32), vm((4, half, TILE), jnp.float32),
            dma, dma((8, PIECES)), dma((8, PIECES)),
            dma((2, 4, 4)), dma((2, 4, 4)), dma((2, 4, 4)), dma((2, 4, 4)),
            dma((2, 4)), dma((2, 4)), dma((2, 4)), dma((2, 4)),
        ],
        compiler_params=pltpu.CompilerParams(
            collective_id=barrier_id, has_side_effects=True, vmem_limit_bytes=60 * 2**20
        ),
    )(table, chosen, sorting, amplitudes, tiles)


def choose(value, cases):
    return sum(jnp.where(value == case, result, 0) for case, result in cases)


def shards(
    amplitudes, integral_tiles, tile_cd, tile_ab, slot_tile, residual_in, occ_level, vir_level
):
    mine = lax.axis_index("vir")
    kinds = amplitudes.shape[1] // TILE
    groups, count = tile_cd.shape
    holders = lax.axis_size("occ")
    part = count // holders // PIECES

    hit = tile_ab[:, :, None] == slot_tile
    slot = jnp.sum(jnp.where(hit, lax.broadcasted_iota(jnp.int32, hit.shape, 2), 0), axis=2)
    group = lax.broadcasted_iota(jnp.int32, slot.shape, 0)
    ox, oz = slot // 16, slot // 4 % 4
    steps = (ox - group // 4 + 4) % 4 * 4 + (oz - group % 4 + 4) % 4
    turn = choose(steps, [(o[0] * 4 + o[1], n) for n, o in enumerate(ORDER)])
    key = (turn * count + lax.broadcasted_iota(jnp.int32, slot.shape, 1)).reshape(groups, holders, -1)
    place = jnp.sum((key[:, :, None, :] < key[:, :, :, None]).astype(jnp.int32), axis=3)
    allowed = choose(turn, [(n, p * part) for n, p in enumerate(EARLY)]).reshape(place.shape)
    crowded = jnp.any(place >= allowed)

    my_place = lax.dynamic_index_in_dim(place, mine, 0, keepdims=False)
    holder = lax.broadcasted_iota(jnp.int32, my_place.shape, 0)
    at = (my_place // part * (holders * part) + holder * part + my_place % part).reshape(-1)
    held = lax.dynamic_index_in_dim(my_place, lax.axis_index("occ"), 0, keepdims=False)
    ordinal = jnp.arange(held.shape[0], dtype=jnp.int32)
    sorting = jnp.sum(jnp.where(held[None, :] == ordinal[:, None], ordinal[None, :], 0), axis=1)

    my_kinds = lax.dynamic_index_in_dim(tile_cd, mine, 0, keepdims=False)
    my_tiles = lax.dynamic_index_in_dim(tile_ab, mine, 0, keepdims=False)
    match = slot_tile[:, None] == my_tiles[None, :]
    number = (at + 1).astype(jnp.float32)[:, None]
    of_kind = jnp.where(my_kinds[:, None] == jnp.arange(kinds, dtype=jnp.int32), number, 0.0)
    named = jnp.dot(match.astype(jnp.float32), of_kind, precision=lax.Precision.HIGHEST).astype(jnp.int32)
    table = jnp.where(named == 0, count, named - 1).reshape(-1)
    r = jnp.any(match, axis=1).reshape(-1, 4)
    least = jnp.where(r[:, 0], 0, jnp.where(r[:, 1], 1, 2))
    most = jnp.where(r[:, 3], 3, jnp.where(r[:, 2], 2, 1))
    chosen = jnp.stack([least, most], axis=1).astype(jnp.int32).reshape(-1)

    tiles = integral_tiles[0]
    by_slot = ladder(EARLY, 0, table, chosen, sorting, amplitudes, tiles)

    def update(value):
        return (residual_in + value) / (occ_level[:, None] - vir_level[None, :])

    return lax.cond(
        crowded,
        lambda: update(ladder(LATE, 1, table, chosen, sorting, amplitudes, tiles)),
        lambda: update(by_slot),
    )


def solution(mesh):
    in_specs = (
        P("occ", "vir"),
        P("vir", "occ", None, None),
        P(),
        P(),
        P(),
        P("occ", "vir"),
        P("occ"),
        P("vir"),
    )
    out_specs = P("occ", "vir")
    return jax.shard_map(shards, mesh=mesh, in_specs=in_specs, out_specs=out_specs, check_vma=False)
```

```python
import functools

import jax
import jax.numpy as jnp
from jax import lax
from jax.experimental import pallas as pl
from jax.experimental.pallas import tpu as pltpu
from jax.sharding import PartitionSpec as P

CAP = 2
TILE = 128
MESH = pl.DeviceIdType.MESH
PIECES = 16
AHEAD = 3
FAR_LAG, LAG = 1, 2
FULL = 32767.0

ORDER = (
    (2, 2), (2, 1), (1, 2), (2, 3), (3, 2), (2, 0), (0, 2), (1, 1),
    (3, 3), (1, 3), (3, 1), (1, 0), (3, 0), (0, 1), (0, 3), (0, 0),
)
EARLY = (5, 7, 8, 10, 11, 12, 13, 14, 15, 15, 16, 16, 16, 16, 16, 16)
LATE = (16,) * 16


def pick(i, values):
    out = jnp.int32(values[0])
    for n, v in enumerate(values[1:], 1):
        out = jnp.where(i == n, jnp.int32(v), out)
    return out


def code(v):
    top = jnp.maximum(jnp.max(jnp.abs(v), axis=0, keepdims=True), 1e-30)
    return jnp.round(v * (FULL / top)).astype(jnp.int32).astype(jnp.int16), top * (1.0 / FULL)


def within(index, size):
    return jnp.minimum(jnp.maximum(index, 0), size - 1)


def cases(value, results):
    out = jnp.zeros_like(value)
    for n, result in enumerate(results):
        out = jnp.where(value == n, result, out)
    return out


def kernel(
    need, slot_tile, tile_ab, tile_cd, amp_hbm, tiles_hbm, out, crowded,
    amp, tiles, sorted_tiles, land, pool, q1s, u1s, q1r, u1r, q2s, u2s, q2r, u2r, own, total,
    slots_v, turns_v, sorting_v, table_v, sorting, table,
    load_sem, gs_send, gs_recv, q1_send, q1_recv, u1_send, u1_recv, q2_send, q2_recv, u2_send, u2_recv,
):
    occ, vir = lax.axis_index("occ"), lax.axis_index("vir")
    y, core = occ // 2, occ % 2
    x, z = vir // 4, vir % 4
    up = (((y + 1) % 4) * 2 + core, vir)
    down = (((y + 3) % 4) * 2 + core, vir)
    mate = (y * 2 + 1 - core, vir)
    at_x = [(occ, ((x + d) % 4) * 4 + z) for d in range(4)]
    at_z = [(occ, x * 4 + (z + d) % 4) for d in range(4)]
    own_tiles = tiles_hbm.shape[0]
    holders = 8
    part = own_tiles // PIECES
    half = amp_hbm.shape[0] // 2
    kinds = amp_hbm.shape[1] // TILE

    load_tiles = pltpu.make_async_copy(tiles_hbm, tiles, load_sem.at[0])
    load_tiles.start()
    load_amp = pltpu.make_async_copy(amp_hbm, amp, load_sem.at[1])
    load_amp.start()

    barrier = pltpu.get_barrier_semaphore()
    greeted = [up, down, mate] + at_x[1:] + at_z[1:]
    for other in greeted:
        pl.semaphore_signal(barrier, inc=1, device_id=other, device_id_type=MESH)

    groups, count = tile_ab.shape
    ab = tile_ab[...]
    slot = jnp.zeros_like(ab)
    for j in range(1, slot_tile.shape[0]):
        slot = jnp.where(ab == slot_tile[j], j, slot)
    group = lax.broadcasted_iota(jnp.int32, ab.shape, 0)
    steps = (slot // 16 - group // 4 + 4) % 4 * 4 + (slot // 4 % 4 - group % 4 + 4) % 4
    turn_of = [ORDER.index((n // 4, n % 4)) for n in range(16)]
    turn = cases(steps, turn_of)
    slots_v[...] = slot
    turns_v[...] = turn

    lane = lax.broadcasted_iota(jnp.int32, (1, count), 1)
    my_slot, my_turn = slots_v[pl.ds(vir, 1)], turns_v[pl.ds(vir, 1)]
    key = ((lane // own_tiles) * 4096 + my_turn * 256 + lane % own_tiles).astype(jnp.float32)
    row = lax.broadcasted_iota(jnp.int32, (count, count), 0)
    column = lax.broadcasted_iota(jnp.int32, (count, count), 1)
    keys = jnp.broadcast_to(key, (count, count))
    key_down = jnp.sum(jnp.where(row == column, keys, 0.0), axis=1, keepdims=True)
    rank = jnp.sum(jnp.where(key_down < keys, 1.0, 0.0), axis=0, keepdims=True).astype(jnp.int32)
    place_row = lax.broadcasted_iota(jnp.int32, (own_tiles, count), 0) + occ * own_tiles
    number = (lane % own_tiles).astype(jnp.float32)
    held = jnp.sum(jnp.where(rank == place_row, number, 0.0), axis=1, keepdims=True)
    sorting_v[...] = jnp.broadcast_to(held, (own_tiles, TILE)).astype(jnp.int32)
    put_sorting = pltpu.make_async_copy(sorting_v, sorting, load_sem.at[2])
    put_sorting.start()
    load_tiles.wait()
    put_sorting.wait()
    for n in range(own_tiles):
        sorted_tiles[n] = tiles[within(sorting[n, 0], own_tiles)]
    pool[pool.shape[0] - 1] = jnp.zeros((TILE, TILE), pool.dtype)
    pl.semaphore_wait(barrier, len(greeted))

    def place(yy, cc, piece, first=0, size=part):
        return land.at[piece, pl.ds(((yy % 4) * 2 + cc) * part + first, size)]

    def send(kind, piece, source, target, device):
        return pltpu.make_async_remote_copy(
            src_ref=source, dst_ref=target, send_sem=gs_send.at[kind, piece],
            recv_sem=gs_recv.at[kind, piece], device_id=device, device_id_type=MESH,
        )

    mid = part // 2

    def mine(p):
        return sorted_tiles.at[pl.ds(p * part, part)]

    def pass_on(kind, p, yy, first, device):
        spot = place(yy, core, p, first, mid)
        return send(kind, p, spot, spot, device)

    def relay(kind, p, yy):
        return send(kind, p, place(yy, core, p), place(yy, core, p), mate)

    def first_up(p):
        return send(0, p, mine(p), place(y, core, p), up)

    def first_down(p):
        return send(1, p, mine(p), place(y, core, p), down)

    def on_up(p):
        return pass_on(2, p, y + 3, 0, up)

    def on_down(p):
        return pass_on(3, p, y + 1, mid, down)

    def to_mate(p):
        return send(4, p, mine(p), place(y, core, p), mate)

    def low_mate(p):
        return relay(5, p, y + 3)

    def high_mate(p):
        return relay(6, p, y + 1)

    def far_mate(p):
        return relay(7, p, y + 2)

    def own_piece(p):
        first_up(p).start()
        first_down(p).start()
        to_mate(p).start()

    def arrive(p):
        first_up(p).wait_recv()
        on_up(p).start()
        low_mate(p).start()
        first_down(p).wait_recv()
        on_down(p).start()
        high_mate(p).start()

        @pl.when(p + AHEAD < PIECES)
        def _():
            own_piece(p + AHEAD)

    def arrive_far(p):
        on_up(p).wait_recv()
        on_down(p).wait_recv()
        far_mate(p).start()

    def complete(p):
        for copies in (to_mate, low_mate, high_mate, far_mate):
            copies(p).wait_recv()
        base = p * part * holders
        pool[pl.ds(base, part * holders)] = land[p]
        pool[pl.ds(base + occ * part, part)] = sorted_tiles[pl.ds(p * part, part)]

    for p in range(AHEAD):
        own_piece(p)

    table_slots = slot_tile.shape[0]
    slot_row = lax.broadcasted_iota(jnp.int32, (table_slots, count), 0)
    match = jnp.where(slot_row == my_slot, 1.0, 0.0).astype(jnp.bfloat16)
    pos = rank % own_tiles
    at = pos // part * (holders * part) + lane // own_tiles * part + pos % part
    kind_row = lax.broadcasted_iota(jnp.int32, (TILE, count), 0)
    of_kind = jnp.where(kind_row == tile_cd[pl.ds(vir, 1)], (at + 1).astype(jnp.float32), 0.0)
    named = lax.dot_general(
        match, of_kind.astype(jnp.bfloat16), (((1,), (1,)), ((), ())), preferred_element_type=jnp.float32
    ).astype(jnp.int32)
    table_v[0:table_slots] = jnp.where(named == 0, count, named - 1)
    reached = jnp.dot(match, jnp.ones((count, TILE), jnp.bfloat16), preferred_element_type=jnp.float32)
    reached = jnp.minimum(reached, 1.0)
    r = lax.broadcasted_iota(jnp.int32, (table_slots, table_slots), 0)
    c = lax.broadcasted_iota(jnp.int32, (table_slots, table_slots), 1)
    before = jnp.where((r // 4 == c // 4) & (c < r), 1.0, 0.0).astype(jnp.bfloat16)
    rank_in = jnp.dot(before, reached.astype(jnp.bfloat16), preferred_element_type=jnp.float32)
    r = lax.broadcasted_iota(jnp.int32, (table_slots, TILE), 0)
    c = lax.broadcasted_iota(jnp.int32, (table_slots, TILE), 1)
    hit = (reached > 0.0) & (r // 4 * CAP + rank_in.astype(jnp.int32) == c)
    chosen = jnp.sum(jnp.where(hit, r.astype(jnp.float32), 0.0), axis=0, keepdims=True)
    table_v[table_slots : table_slots + 8] = jnp.broadcast_to(chosen, (8, TILE)).astype(jnp.int32)
    put_table = pltpu.make_async_copy(table_v, table, load_sem.at[2])
    put_table.start()

    a = lax.broadcasted_iota(jnp.int32, (count, TILE), 0)
    c = lax.broadcasted_iota(jnp.int32, (count, TILE), 1)
    holds = jnp.where(a // own_tiles == c, 1.0, 0.0).astype(jnp.bfloat16)
    turn = turns_v[...]
    worst = jnp.zeros((groups, TILE), jnp.float32)
    for n, pieces in enumerate(need):
        if pieces < PIECES:
            early = jnp.where(turn <= n, 1.0, 0.0).astype(jnp.bfloat16)
            tally = jnp.dot(early, holds, preferred_element_type=jnp.float32)
            worst = jnp.maximum(worst, tally - pieces * part)
    worst = jnp.max(jnp.max(worst, axis=1, keepdims=True), axis=0, keepdims=True)
    crowded[...] = jnp.broadcast_to(worst, crowded.shape)
    put_table.wait()
    load_amp.wait()

    def first_leg(h, d, e):
        device = (occ, ((x + d) % 4) * 4 + z) if h == 0 else (occ, x * 4 + (z + d) % 4)
        return [
            pltpu.make_async_remote_copy(
                src_ref=s.at[h, d, e], dst_ref=r.at[h, d, e], send_sem=ss.at[h, d, e],
                recv_sem=rs.at[h, d, e], device_id=device, device_id_type=MESH,
            )
            for s, r, ss, rs in ((q1s, q1r, q1_send, q1_recv), (u1s, u1r, u1_send, u1_recv))
        ]

    rows4 = lax.broadcasted_iota(jnp.int32, (4, TILE), 0)

    def one_owner(i, carry):
        dx, dz = pick(i, [o[0] for o in ORDER]), pick(i, [o[1] for o in ORDER])
        owner = ((x + dx) % 4) * 4 + (z + dz) % 4
        slots = [within(table[table_slots, owner * CAP + b], table_slots) for b in range(CAP)]
        value = jnp.zeros((2 * half, CAP * TILE), jnp.float32)
        for k in range(0, kinds, 2):
            rhs = jnp.concatenate(
                [
                    jnp.concatenate([pool[within(table[slots[b], kk], count + 1)] for b in range(CAP)], axis=1)
                    for kk in (k, k + 1)
                ],
                axis=0,
            )
            value = value + jnp.dot(
                amp[:, k * TILE : (k + 2) * TILE], rhs, preferred_element_type=jnp.float32
            )
        for h, d, e in ((0, dx, dz), (1, dz, dx)):
            units = []
            for b in range(CAP):
                q, unit = code(value[h * half : (h + 1) * half, b * TILE : (b + 1) * TILE])
                q1s[h, d, e, b] = q
                units.append(jnp.where(rows4 == slots[b] - owner * 4, unit, 0.0))
            u1s[h, d, e] = jnp.concatenate(units, axis=0)

            @pl.when(d != 0)
            def _():
                for copy in first_leg(h, d, e):
                    copy.start()

        return carry

    def second_leg(h, e):
        near = at_z if h == 0 else at_x
        pairs = ((e, 0, 4),) if e != 2 else ((1, 0, 2), (3, 2, 2))
        return [
            pltpu.make_async_remote_copy(
                src_ref=s.at[h, e, pl.ds(first, size)] if s is q2s else s.at[h, e],
                dst_ref=r.at[h, e, pl.ds(first, size)] if r is q2r else r.at[h, e if e != 2 else e - 2 + first],
                send_sem=ss.at[h, e if to == e else first], recv_sem=rs.at[h, e if to == e else first],
                device_id=near[to], device_id_type=MESH,
            )
            for to, first, size in pairs
            for s, r, ss, rs in ((q2s, q2r, q2_send, q2_recv), (u2s, u2r, u2_send, u2_recv))
        ]

    step = 64

    def add_up(h, e, into):
        for d in range(1, 4):
            for copy in first_leg(h, d, e):
                copy.wait_recv()

        def some_rows(n, carry):
            span = pl.ds(pl.multiple_of(n * step, step), step)
            sums = [jnp.zeros((step, TILE), jnp.float32) for _ in range(4)]
            for d in range(4):
                q_ref, u_ref = (q1s, u1s) if d == 0 else (q1r, u1r)
                for b in range(CAP):
                    v = q_ref[h, d, e, b, span].astype(jnp.int32).astype(jnp.float32)
                    for j in range(4):
                        row = b * 4 + j
                        sums[j] = sums[j] + v * u_ref[h, d, e, row : row + 1]
            for j in range(4):
                into[j, span] = sums[j]
            return carry

        lax.fori_loop(0, half // step, some_rows, 0)

    def second(e):
        for h in range(2):
            add_up(h, e, total)
            if e != 2:
                first = 0 if e == 1 else 2
                for copy in second_leg(h, 2)[first : first + 2]:
                    copy.wait_recv()
                for j in (first, first + 1):
                    passing = q2r[h, 2, j].astype(jnp.int32).astype(jnp.float32)
                    total[j] = total[j] + passing * u2r[h, first, j : j + 1]
            units = []
            for j in range(4):
                q, unit = code(total[j])
                q2s[h, e, j] = q
                units.append(unit)
            u2s[h, e] = jnp.concatenate(units + units, axis=0)
            for copy in second_leg(h, e):
                copy.start()

    early_second = need[6] + LAG + 1 if need[6] < PIECES else None

    def one_piece(p, done):
        @pl.when(p < PIECES)
        def _():
            arrive(p)

        if early_second is not None:

            @pl.when(p == early_second)
            def _():
                second(2)

        @pl.when(p >= LAG)
        def _():
            complete(p - LAG)

        ready = jnp.int32(0)
        for n in need:
            ready = ready + jnp.where(p >= n + LAG - 1, 1, 0)
        lax.fori_loop(done, ready, one_owner, 0)
        @pl.when((p >= FAR_LAG) & (p < PIECES + FAR_LAG))
        def _():
            arrive_far(p - FAR_LAG)

        return ready

    lax.fori_loop(0, PIECES + LAG, one_piece, jnp.int32(0))
    if early_second is None:
        second(2)
    second(1)
    second(3)
    for h in range(2):
        add_up(h, 0, own.at[h])
    for h in range(2):
        for e in (1, 3):
            for copy in second_leg(h, e):
                copy.wait_recv()

    for h in range(2):

        def finish(n, carry):
            span = pl.ds(pl.multiple_of(n * step, step), step)
            rows = pl.ds(pl.multiple_of(h * half + n * step, step), step)
            for j in range(4):
                v = own[h, j, span]
                for e in (1, 3):
                    v = v + q2r[h, e, j, span].astype(jnp.int32).astype(jnp.float32) * u2r[h, e, j : j + 1]
                out[rows, j * TILE : (j + 1) * TILE] = v
            return carry

        lax.fori_loop(0, half // step, finish, 0)

    def all_sent(p, carry):
        for copies in (first_up, first_down, on_up, on_down, to_mate, low_mate, high_mate, far_mate):
            copies(p).wait_send()
        return carry

    lax.fori_loop(0, PIECES, all_sent, 0)
    for h in range(2):
        for e in range(4):
            for d in range(1, 4):
                for copy in first_leg(h, d, e):
                    copy.wait_send()
            if e:
                for copy in second_leg(h, e):
                    copy.wait_send()


def ladder(need, barrier_id, slot_tile, tile_ab, tile_cd, amplitudes, tiles):
    rows = amplitudes.shape[0]
    half, every = rows // 2, tiles.shape[0] * 8
    vm, dma = pltpu.VMEM, pltpu.SemaphoreType.DMA
    first_q, first_u = (2, 4, 4, CAP, half, TILE), (2, 4, 4, 8, TILE)
    second_q, second_u = (2, 4, 4, half, TILE), (2, 4, 8, TILE)
    rows_of_table = slot_tile.shape[0] + 8
    return pl.pallas_call(
        functools.partial(kernel, need),
        out_shape=(
            jax.ShapeDtypeStruct((rows, 4 * TILE), jnp.float32),
            jax.ShapeDtypeStruct((8, TILE), jnp.float32),
        ),
        in_specs=[
            pl.BlockSpec(memory_space=pltpu.SMEM),
            pl.BlockSpec(memory_space=pltpu.VMEM),
            pl.BlockSpec(memory_space=pltpu.VMEM),
            pl.BlockSpec(memory_space=pl.ANY),
            pl.BlockSpec(memory_space=pl.ANY),
        ],
        out_specs=(pl.BlockSpec(memory_space=pltpu.VMEM), pl.BlockSpec(memory_space=pltpu.VMEM)),
        scratch_shapes=[
            vm(amplitudes.shape, jnp.bfloat16),
            vm(tiles.shape, jnp.bfloat16),
            vm(tiles.shape, jnp.bfloat16),
            vm((PIECES, every // PIECES, TILE, TILE), jnp.bfloat16),
            vm((every + 1, TILE, TILE), jnp.bfloat16),
            vm(first_q, jnp.int16), vm(first_u, jnp.float32), vm(first_q, jnp.int16), vm(first_u, jnp.float32),
            vm(second_q, jnp.int16), vm(second_u, jnp.float32), vm(second_q, jnp.int16), vm(second_u, jnp.float32),
            vm((2, 4, half, TILE), jnp.float32), vm((4, half, TILE), jnp.float32),
            vm(tile_ab.shape, jnp.int32), vm(tile_ab.shape, jnp.int32),
            vm((tiles.shape[0], TILE), jnp.int32), vm((rows_of_table, TILE), jnp.int32),
            pltpu.SMEM((tiles.shape[0], TILE), jnp.int32), pltpu.SMEM((rows_of_table, TILE), jnp.int32),
            dma((3,)), dma((8, PIECES)), dma((8, PIECES)),
            dma((2, 4, 4)), dma((2, 4, 4)), dma((2, 4, 4)), dma((2, 4, 4)),
            dma((2, 4)), dma((2, 4)), dma((2, 4)), dma((2, 4)),
        ],
        compiler_params=pltpu.CompilerParams(
            collective_id=barrier_id, has_side_effects=True, vmem_limit_bytes=60 * 2**20
        ),
    )(slot_tile, tile_ab, tile_cd, amplitudes, tiles)


def shards(
    amplitudes, integral_tiles, tile_cd, tile_ab, slot_tile, residual_in, occ_level, vir_level
):
    operands = (slot_tile, tile_ab, tile_cd, amplitudes, integral_tiles[0])
    by_slot, crowded = ladder(EARLY, 0, *operands)

    def update(value):
        return (residual_in + value) / (occ_level[:, None] - vir_level[None, :])

    return lax.cond(
        crowded[0, 0] > 0.0,
        lambda: update(ladder(LATE, 1, *operands)[0]),
        lambda: update(by_slot),
    )


def solution(mesh):
    in_specs = (
        P("occ", "vir"),
        P("vir", "occ", None, None),
        P(),
        P(),
        P(),
        P("occ", "vir"),
        P("occ"),
        P("vir"),
    )
    out_specs = P("occ", "vir")
    return jax.shard_map(shards, mesh=mesh, in_specs=in_specs, out_specs=out_specs, check_vma=False)
```

```python
import functools

import jax
import jax.numpy as jnp
from jax import lax
from jax.experimental import pallas as pl
from jax.experimental.pallas import tpu as pltpu
from jax.sharding import PartitionSpec as P

CAP = 2
TILE = 128
MESH = pl.DeviceIdType.MESH
PIECES = 16
AHEAD = 3
FAR_LAG, LAG = 1, 2
FULL = 32767.0

ORDER = (
    (2, 2), (2, 1), (1, 2), (2, 3), (3, 2), (2, 0), (0, 2), (1, 1),
    (3, 3), (1, 3), (3, 1), (1, 0), (3, 0), (0, 1), (0, 3), (0, 0),
)
EARLY = (5, 7, 8, 10, 11, 12, 13, 14, 15, 15, 16, 16, 16, 16, 16, 16)
LATE = (16,) * 16


def pick(i, values):
    out = jnp.int32(values[0])
    for n, v in enumerate(values[1:], 1):
        out = jnp.where(i == n, jnp.int32(v), out)
    return out


def code(v):
    top = jnp.maximum(jnp.max(jnp.abs(v), axis=0, keepdims=True), 1e-30)
    return jnp.round(v * (FULL / top)).astype(jnp.int32).astype(jnp.int16), top * (1.0 / FULL)


def within(index, size):
    return jnp.minimum(jnp.maximum(index, 0), size - 1)


def cases(value, results):
    out = jnp.zeros_like(value)
    for n, result in enumerate(results):
        out = jnp.where(value == n, result, out)
    return out


def kernel(
    need, slot_tile, tile_ab, tile_cd, amp_hbm, tiles_hbm, out, crowded,
    amp, tiles, sorted_tiles, land, pool, q1s, u1s, q1r, u1r, q2s, u2s, q2r, u2r, own, total,
    slots_v, turns_v, sorting_v, table_v, sorting, table,
    load_sem, gs_send, gs_recv, q1_send, q1_recv, u1_send, u1_recv, q2_send, q2_recv, u2_send, u2_recv,
):
    occ, vir = lax.axis_index("occ"), lax.axis_index("vir")
    y, core = occ // 2, occ % 2
    x, z = vir // 4, vir % 4
    up = (((y + 1) % 4) * 2 + core, vir)
    down = (((y + 3) % 4) * 2 + core, vir)
    mate = (y * 2 + 1 - core, vir)
    at_x = [(occ, ((x + d) % 4) * 4 + z) for d in range(4)]
    at_z = [(occ, x * 4 + (z + d) % 4) for d in range(4)]
    own_tiles = tiles_hbm.shape[0]
    holders = 8
    part = own_tiles // PIECES
    half = amp_hbm.shape[0] // 2
    kinds = amp_hbm.shape[1] // TILE

    load_tiles = pltpu.make_async_copy(tiles_hbm, tiles, load_sem.at[0])
    load_tiles.start()
    load_amp = pltpu.make_async_copy(amp_hbm, amp, load_sem.at[1])
    load_amp.start()

    barrier = pltpu.get_barrier_semaphore()
    greeted = [up, down, mate] + at_x[1:] + at_z[1:]
    for other in greeted:
        pl.semaphore_signal(barrier, inc=1, device_id=other, device_id_type=MESH)

    groups, count = tile_ab.shape
    ab = tile_ab[...]
    slot = jnp.zeros_like(ab)
    for j in range(1, slot_tile.shape[0]):
        slot = jnp.where(ab == slot_tile[j], j, slot)
    group = lax.broadcasted_iota(jnp.int32, ab.shape, 0)
    steps = (slot // 16 - group // 4 + 4) % 4 * 4 + (slot // 4 % 4 - group % 4 + 4) % 4
    turn_of = [ORDER.index((n // 4, n % 4)) for n in range(16)]
    turn = cases(steps, turn_of)
    slots_v[...] = slot
    turns_v[...] = turn

    lane = lax.broadcasted_iota(jnp.int32, (1, count), 1)
    my_slot, my_turn = slots_v[pl.ds(vir, 1)], turns_v[pl.ds(vir, 1)]
    key = ((lane // own_tiles) * 4096 + my_turn * 256 + lane % own_tiles).astype(jnp.float32)
    row = lax.broadcasted_iota(jnp.int32, (count, count), 0)
    column = lax.broadcasted_iota(jnp.int32, (count, count), 1)
    keys = jnp.broadcast_to(key, (count, count))
    key_down = jnp.sum(jnp.where(row == column, keys, 0.0), axis=1, keepdims=True)
    rank = jnp.sum(jnp.where(key_down < keys, 1.0, 0.0), axis=0, keepdims=True).astype(jnp.int32)
    place_row = lax.broadcasted_iota(jnp.int32, (own_tiles, count), 0) + occ * own_tiles
    number = (lane % own_tiles).astype(jnp.float32)
    held = jnp.sum(jnp.where(rank == place_row, number, 0.0), axis=1, keepdims=True)
    sorting_v[...] = jnp.broadcast_to(held, (own_tiles, TILE)).astype(jnp.int32)
    put_sorting = pltpu.make_async_copy(sorting_v, sorting, load_sem.at[2])
    put_sorting.start()
    load_tiles.wait()
    put_sorting.wait()
    for n in range(own_tiles):
        sorted_tiles[n] = tiles[within(sorting[n, 0], own_tiles)]
    pool[pool.shape[0] - 1] = jnp.zeros((TILE, TILE), pool.dtype)
    pl.semaphore_wait(barrier, len(greeted))

    def place(yy, cc, piece, first=0, size=part):
        return land.at[piece, pl.ds(((yy % 4) * 2 + cc) * part + first, size)]

    def send(kind, piece, source, target, device):
        return pltpu.make_async_remote_copy(
            src_ref=source, dst_ref=target, send_sem=gs_send.at[kind, piece],
            recv_sem=gs_recv.at[kind, piece], device_id=device, device_id_type=MESH,
        )

    mid = part // 2

    def mine(p):
        return sorted_tiles.at[pl.ds(p * part, part)]

    def pass_on(kind, p, yy, first, device):
        spot = place(yy, core, p, first, mid)
        return send(kind, p, spot, spot, device)

    def relay(kind, p, yy):
        return send(kind, p, place(yy, core, p), place(yy, core, p), mate)

    def first_up(p):
        return send(0, p, mine(p), place(y, core, p), up)

    def first_down(p):
        return send(1, p, mine(p), place(y, core, p), down)

    def on_up(p):
        return pass_on(2, p, y + 3, 0, up)

    def on_down(p):
        return pass_on(3, p, y + 1, mid, down)

    def to_mate(p):
        return send(4, p, mine(p), place(y, core, p), mate)

    def low_mate(p):
        return relay(5, p, y + 3)

    def high_mate(p):
        return relay(6, p, y + 1)

    def far_mate(p):
        return relay(7, p, y + 2)

    def own_piece(p):
        first_up(p).start()
        first_down(p).start()
        to_mate(p).start()

    def arrive(p):
        first_up(p).wait_recv()
        on_up(p).start()
        low_mate(p).start()
        first_down(p).wait_recv()
        on_down(p).start()
        high_mate(p).start()

        @pl.when(p + AHEAD < PIECES)
        def _():
            own_piece(p + AHEAD)

    def arrive_far(p):
        on_up(p).wait_recv()
        on_down(p).wait_recv()
        far_mate(p).start()

    def complete(p):
        for copies in (to_mate, low_mate, high_mate, far_mate):
            copies(p).wait_recv()
        base = p * part * holders
        pool[pl.ds(base, part * holders)] = land[p]
        pool[pl.ds(base + occ * part, part)] = sorted_tiles[pl.ds(p * part, part)]

    for p in range(AHEAD):
        own_piece(p)

    table_slots = slot_tile.shape[0]
    slot_row = lax.broadcasted_iota(jnp.int32, (table_slots, count), 0)
    match = jnp.where(slot_row == my_slot, 1.0, 0.0).astype(jnp.bfloat16)
    pos = rank % own_tiles
    at = pos // part * (holders * part) + lane // own_tiles * part + pos % part
    kind_row = lax.broadcasted_iota(jnp.int32, (TILE, count), 0)
    of_kind = jnp.where(kind_row == tile_cd[pl.ds(vir, 1)], (at + 1).astype(jnp.float32), 0.0)
    named = lax.dot_general(
        match, of_kind.astype(jnp.bfloat16), (((1,), (1,)), ((), ())), preferred_element_type=jnp.float32
    ).astype(jnp.int32)
    table_v[0:table_slots] = jnp.where(named == 0, count, named - 1)
    reached = jnp.dot(match, jnp.ones((count, TILE), jnp.bfloat16), preferred_element_type=jnp.float32)
    reached = jnp.minimum(reached, 1.0)
    r = lax.broadcasted_iota(jnp.int32, (table_slots, table_slots), 0)
    c = lax.broadcasted_iota(jnp.int32, (table_slots, table_slots), 1)
    before = jnp.where((r // 4 == c // 4) & (c < r), 1.0, 0.0).astype(jnp.bfloat16)
    rank_in = jnp.dot(before, reached.astype(jnp.bfloat16), preferred_element_type=jnp.float32)
    r = lax.broadcasted_iota(jnp.int32, (table_slots, TILE), 0)
    c = lax.broadcasted_iota(jnp.int32, (table_slots, TILE), 1)
    hit = (reached > 0.0) & (r // 4 * CAP + rank_in.astype(jnp.int32) == c)
    chosen = jnp.sum(jnp.where(hit, r.astype(jnp.float32), 0.0), axis=0, keepdims=True)
    table_v[table_slots : table_slots + 8] = jnp.broadcast_to(chosen, (8, TILE)).astype(jnp.int32)
    put_table = pltpu.make_async_copy(table_v, table, load_sem.at[2])
    put_table.start()

    a = lax.broadcasted_iota(jnp.int32, (count, TILE), 0)
    c = lax.broadcasted_iota(jnp.int32, (count, TILE), 1)
    holds = jnp.where(a // own_tiles == c, 1.0, 0.0).astype(jnp.bfloat16)
    turn = turns_v[...]
    worst = jnp.zeros((groups, TILE), jnp.float32)
    for n, pieces in enumerate(need):
        if pieces < PIECES:
            early = jnp.where(turn <= n, 1.0, 0.0).astype(jnp.bfloat16)
            tally = jnp.dot(early, holds, preferred_element_type=jnp.float32)
            worst = jnp.maximum(worst, tally - pieces * part)
    worst = jnp.max(jnp.max(worst, axis=1, keepdims=True), axis=0, keepdims=True)
    crowded[...] = jnp.broadcast_to(worst, crowded.shape)
    put_table.wait()
    load_amp.wait()

    def first_leg(h, d, e):
        device = (occ, ((x + d) % 4) * 4 + z) if h == 0 else (occ, x * 4 + (z + d) % 4)
        return [
            pltpu.make_async_remote_copy(
                src_ref=s.at[h, d, e], dst_ref=r.at[h, d, e], send_sem=ss.at[h, d, e],
                recv_sem=rs.at[h, d, e], device_id=device, device_id_type=MESH,
            )
            for s, r, ss, rs in ((q1s, q1r, q1_send, q1_recv), (u1s, u1r, u1_send, u1_recv))
        ]

    rows4 = lax.broadcasted_iota(jnp.int32, (4, TILE), 0)

    def one_owner(i, carry):
        dx, dz = pick(i, [o[0] for o in ORDER]), pick(i, [o[1] for o in ORDER])
        owner = ((x + dx) % 4) * 4 + (z + dz) % 4
        slots = [within(table[table_slots, owner * CAP + b], table_slots) for b in range(CAP)]
        value = jnp.zeros((2 * half, CAP * TILE), jnp.float32)
        for k in range(0, kinds, 2):
            rhs = jnp.concatenate(
                [
                    jnp.concatenate([pool[within(table[slots[b], kk], count + 1)] for b in range(CAP)], axis=1)
                    for kk in (k, k + 1)
                ],
                axis=0,
            )
            value = value + jnp.dot(
                amp[:, k * TILE : (k + 2) * TILE], rhs, preferred_element_type=jnp.float32
            )
        for h, d, e in ((0, dx, dz), (1, dz, dx)):
            units = []
            for b in range(CAP):
                q, unit = code(value[h * half : (h + 1) * half, b * TILE : (b + 1) * TILE])
                q1s[h, d, e, b] = q
                units.append(jnp.where(rows4 == slots[b] - owner * 4, unit, 0.0))
            u1s[h, d, e] = jnp.concatenate(units, axis=0)

            @pl.when(d != 0)
            def _():
                for copy in first_leg(h, d, e):
                    copy.start()

        return carry

    def second_leg(h, e):
        near = at_z if h == 0 else at_x
        pairs = ((e, 0, 4),) if e != 2 else ((1, 0, 2), (3, 2, 2))
        return [
            pltpu.make_async_remote_copy(
                src_ref=s.at[h, e, pl.ds(first, size)] if s is q2s else s.at[h, e],
                dst_ref=r.at[h, e, pl.ds(first, size)] if r is q2r else r.at[h, e if e != 2 else e - 2 + first],
                send_sem=ss.at[h, e if to == e else first], recv_sem=rs.at[h, e if to == e else first],
                device_id=near[to], device_id_type=MESH,
            )
            for to, first, size in pairs
            for s, r, ss, rs in ((q2s, q2r, q2_send, q2_recv), (u2s, u2r, u2_send, u2_recv))
        ]

    step = 64

    def add_up(h, e, into):
        for d in range(1, 4):
            for copy in first_leg(h, d, e):
                copy.wait_recv()

        def some_rows(n, carry):
            span = pl.ds(pl.multiple_of(n * step, step), step)
            sums = [jnp.zeros((step, TILE), jnp.float32) for _ in range(4)]
            for d in range(4):
                q_ref, u_ref = (q1s, u1s) if d == 0 else (q1r, u1r)
                for b in range(CAP):
                    v = q_ref[h, d, e, b, span].astype(jnp.int32).astype(jnp.float32)
                    for j in range(4):
                        row = b * 4 + j
                        sums[j] = sums[j] + v * u_ref[h, d, e, row : row + 1]
            for j in range(4):
                into[j, span] = sums[j]
            return carry

        lax.fori_loop(0, half // step, some_rows, 0)

    def second(e):
        for h in range(2):
            add_up(h, e, total)
            if e != 2:
                first = 0 if e == 1 else 2
                for copy in second_leg(h, 2)[first : first + 2]:
                    copy.wait_recv()
                for j in (first, first + 1):
                    passing = q2r[h, 2, j].astype(jnp.int32).astype(jnp.float32)
                    total[j] = total[j] + passing * u2r[h, first, j : j + 1]
            units = []
            for j in range(4):
                q, unit = code(total[j])
                q2s[h, e, j] = q
                units.append(unit)
            u2s[h, e] = jnp.concatenate(units + units, axis=0)
            for copy in second_leg(h, e):
                copy.start()

    early_second = need[6] + LAG + 1 if need[6] < PIECES else None

    def one_piece(p, done):
        @pl.when(p < PIECES)
        def _():
            arrive(p)

        if early_second is not None:

            @pl.when(p == early_second)
            def _():
                second(2)

        @pl.when(p >= LAG)
        def _():
            complete(p - LAG)

        ready = jnp.int32(0)
        for n in need:
            ready = ready + jnp.where(p >= n + LAG - 1, 1, 0)
        lax.fori_loop(done, ready, one_owner, 0)
        @pl.when((p >= FAR_LAG) & (p < PIECES + FAR_LAG))
        def _():
            arrive_far(p - FAR_LAG)

        return ready

    lax.fori_loop(0, PIECES + LAG, one_piece, jnp.int32(0))
    if early_second is None:
        second(2)
    second(1)
    second(3)
    for h in range(2):
        add_up(h, 0, own.at[h])
    for h in range(2):
        for e in (1, 3):
            for copy in second_leg(h, e):
                copy.wait_recv()

        def finish(n, carry):
            span = pl.ds(pl.multiple_of(n * step, step), step)
            rows = pl.ds(pl.multiple_of(h * half + n * step, step), step)
            for j in range(4):
                v = own[h, j, span]
                for e in (1, 3):
                    v = v + q2r[h, e, j, span].astype(jnp.int32).astype(jnp.float32) * u2r[h, e, j : j + 1]
                out[rows, j * TILE : (j + 1) * TILE] = v
            return carry

        lax.fori_loop(0, half // step, finish, 0)

    def all_sent(p, carry):
        for copies in (first_up, first_down, on_up, on_down, to_mate, low_mate, high_mate, far_mate):
            copies(p).wait_send()
        return carry

    lax.fori_loop(0, PIECES, all_sent, 0)
    for h in range(2):
        for e in range(4):
            for d in range(1, 4):
                for copy in first_leg(h, d, e):
                    copy.wait_send()
            if e:
                for copy in second_leg(h, e):
                    copy.wait_send()


def ladder(need, barrier_id, slot_tile, tile_ab, tile_cd, amplitudes, tiles):
    rows = amplitudes.shape[0]
    half, every = rows // 2, tiles.shape[0] * 8
    vm, dma = pltpu.VMEM, pltpu.SemaphoreType.DMA
    first_q, first_u = (2, 4, 4, CAP, half, TILE), (2, 4, 4, 8, TILE)
    second_q, second_u = (2, 4, 4, half, TILE), (2, 4, 8, TILE)
    rows_of_table = slot_tile.shape[0] + 8
    return pl.pallas_call(
        functools.partial(kernel, need),
        out_shape=(
            jax.ShapeDtypeStruct((rows, 4 * TILE), jnp.float32),
            jax.ShapeDtypeStruct((8, TILE), jnp.float32),
        ),
        in_specs=[
            pl.BlockSpec(memory_space=pltpu.SMEM),
            pl.BlockSpec(memory_space=pltpu.VMEM),
            pl.BlockSpec(memory_space=pltpu.VMEM),
            pl.BlockSpec(memory_space=pl.ANY),
            pl.BlockSpec(memory_space=pl.ANY),
        ],
        out_specs=(pl.BlockSpec(memory_space=pltpu.VMEM), pl.BlockSpec(memory_space=pltpu.VMEM)),
        scratch_shapes=[
            vm(amplitudes.shape, jnp.bfloat16),
            vm(tiles.shape, jnp.bfloat16),
            vm(tiles.shape, jnp.bfloat16),
            vm((PIECES, every // PIECES, TILE, TILE), jnp.bfloat16),
            vm((every + 1, TILE, TILE), jnp.bfloat16),
            vm(first_q, jnp.int16), vm(first_u, jnp.float32), vm(first_q, jnp.int16), vm(first_u, jnp.float32),
            vm(second_q, jnp.int16), vm(second_u, jnp.float32), vm(second_q, jnp.int16), vm(second_u, jnp.float32),
            vm((2, 4, half, TILE), jnp.float32), vm((4, half, TILE), jnp.float32),
            vm(tile_ab.shape, jnp.int32), vm(tile_ab.shape, jnp.int32),
            vm((tiles.shape[0], TILE), jnp.int32), vm((rows_of_table, TILE), jnp.int32),
            pltpu.SMEM((tiles.shape[0], TILE), jnp.int32), pltpu.SMEM((rows_of_table, TILE), jnp.int32),
            dma((3,)), dma((8, PIECES)), dma((8, PIECES)),
            dma((2, 4, 4)), dma((2, 4, 4)), dma((2, 4, 4)), dma((2, 4, 4)),
            dma((2, 4)), dma((2, 4)), dma((2, 4)), dma((2, 4)),
        ],
        compiler_params=pltpu.CompilerParams(
            collective_id=barrier_id, has_side_effects=True, vmem_limit_bytes=60 * 2**20
        ),
    )(slot_tile, tile_ab, tile_cd, amplitudes, tiles)


def shards(
    amplitudes, integral_tiles, tile_cd, tile_ab, slot_tile, residual_in, occ_level, vir_level
):
    operands = (slot_tile, tile_ab, tile_cd, amplitudes, integral_tiles[0])
    by_slot, crowded = ladder(EARLY, 0, *operands)

    def update(value):
        return (residual_in + value) / (occ_level[:, None] - vir_level[None, :])

    return lax.cond(
        crowded[0, 0] > 0.0,
        lambda: update(ladder(LATE, 1, *operands)[0]),
        lambda: update(by_slot),
    )


def solution(mesh):
    in_specs = (
        P("occ", "vir"),
        P("vir", "occ", None, None),
        P(),
        P(),
        P(),
        P("occ", "vir"),
        P("occ"),
        P("vir"),
    )
    out_specs = P("occ", "vir")
    return jax.shard_map(shards, mesh=mesh, in_specs=in_specs, out_specs=out_specs, check_vma=False)
```
